512 devices in a mesh: src: 16 (over z, core), tgt: 32 (over x, y).
Axes of the slice: x: 4, y: 8, z: 8, core: 2. Of those that a mesh axis runs over, the one named last changes fastest.
Arguments:
- source_points: bfloat16 [32, 32768], P(None, 'src'), may hold values from -20 to 20
- target_points: bfloat16 [32, 32768], P(None, 'tgt'), may hold values from -20 to 20
- source_mass: float32 [32768], P('src'), may hold values from -1.5 to 1.5
- target_mass: float32 [32768], P('tgt'), may hold values from -1.5 to 1.5
- target_start: float32 [32768], P('tgt'), may hold values from -3 to 131
Outputs:
- source_potential: float32 [32768], P('src')
- target_potential: float32 [32768], P('tgt')
- mapped_cells: float32 [32, 32768], P(None, 'src')
The draws below stay inside these ranges and needn't reach their ends.
All inputs are finite; a program needn't handle non-finite values.
Results may differ from the reference program's by a relative error of at most 0.0003.
Values sent between devices are 32-bit elements; how exact they have to be, the bound alone decides.
A program may use at most 64 MiB of HBM per device.

```python
import math
import jax
import jax.numpy as jnp
from jax import lax

DIM = 32
T_DEV = 1024
ITERS = 2
NSRC = 32768
NTGT = 32768


def cluster_centers(key):
    return 0.2 * jax.random.normal(jax.random.fold_in(key, 101), (64, DIM), jnp.float32)


def draw_source_points(key, part):
    centers = cluster_centers(key)
    own_key = jax.random.fold_in(key, 1)
    labels = jax.random.randint(jax.random.fold_in(own_key, 7), (NSRC,), 0, 64)
    spread = jnp.exp(jax.random.uniform(jax.random.fold_in(own_key, 1), (NSRC,), jnp.float32, math.log(0.2), math.log(0.4)))
    noise = jax.random.normal(jax.random.fold_in(own_key, 2), (NSRC, DIM), jnp.float32)
    points = centers[labels] + spread[:, None] * noise
    return jnp.clip(points, -20.0, 20.0).T.astype(jnp.bfloat16)


def draw_target_points(key, part):
    centers = cluster_centers(key)
    own_key = jax.random.fold_in(key, 2)
    labels = jax.random.randint(jax.random.fold_in(own_key, 7), (NTGT,), 0, 64)
    drift = 0.15 * jax.random.normal(jax.random.fold_in(own_key, 1), (64, DIM), jnp.float32)
    spread = jnp.exp(jax.random.uniform(jax.random.fold_in(own_key, 2), (NTGT,), jnp.float32, math.log(0.2), math.log(0.4)))
    noise = jax.random.normal(jax.random.fold_in(own_key, 3), (NTGT, DIM), jnp.float32)
    points = centers[labels] + drift[labels] + spread[:, None] * noise
    return jnp.clip(points, -20.0, 20.0).T.astype(jnp.bfloat16)


def draw_target_start(key, part):
    own_key = jax.random.fold_in(key, 3)
    return jnp.clip(0.5 * jax.random.normal(own_key, (NTGT,), jnp.float32), -3.0, 3.0)


def shard_levels(key, extent, split, least, top_value):
    gain = 1.0
    for dim, parts in split:
        draws = jax.random.uniform(jax.random.fold_in(jax.random.fold_in(key, 6), dim), (parts,), jnp.float32, least / len(split), top_value / len(split))
        gain = gain * jnp.repeat(jnp.exp(draws), extent[dim] // parts).reshape((-1,) + (1,) * (len(extent) - 1 - dim))
    return gain


def setup_inputs(seed: int = 0) -> dict:
    key_list = jax.random.split(jax.random.key(seed), 6)
    source_points = draw_source_points(jax.random.fold_in(key_list[5], 71), 0)
    target_points = draw_target_points(jax.random.fold_in(key_list[5], 71), 0)
    source_mass = jnp.clip(jax.random.uniform(key_list[2], (NSRC,), jnp.float32, -1.5, 1.5) * shard_levels(key_list[2], (NSRC,), ((0, 16),), -0.4, 0.0), -1.5, 1.5)
    target_mass = jnp.clip(jax.random.uniform(key_list[3], (NTGT,), jnp.float32, -1.5, 1.5) * shard_levels(key_list[3], (NTGT,), ((0, 32),), -0.4, 0.0), -1.5, 1.5)
    target_start = draw_target_start(jax.random.fold_in(key_list[5], 71), 0)
    return dict(source_points=source_points, target_points=target_points, source_mass=source_mass, target_mass=target_mass, target_start=target_start)


entropic_blur = 0.5


def point_squares(points):
    return jnp.sum(jnp.square(points.astype(jnp.float32)), axis=0)


def pair_distances(points, squares, others, other_squares):
    inner_products = jnp.dot(points.T, others, preferred_element_type=jnp.float32)
    return squares[:, None] + other_squares[None, :] - 2.0 * inner_products


def source_update(source_points, source_squares, target_points, target_squares, column_terms):
    row_count = source_points.shape[1]
    block_rows = math.gcd(row_count, 1024)

    def one_block(offset):
        source_piece = lax.dynamic_slice_in_dim(source_points, offset, block_rows, 1)
        piece_squares = lax.dynamic_slice_in_dim(source_squares, offset, block_rows, 0)
        scores = column_terms[None, :] - pair_distances(source_piece, piece_squares, target_points, target_squares) / entropic_blur
        return -entropic_blur * jax.nn.logsumexp(scores, axis=1)

    offsets = jnp.arange(row_count // block_rows, dtype=jnp.int32) * block_rows
    return lax.map(one_block, offsets).reshape(row_count)


def target_update(source_points, source_squares, row_terms, target_points, target_squares):
    columns = target_points.shape[1]
    block_columns = math.gcd(columns, 1024)

    def one_block(offset):
        target_piece = lax.dynamic_slice_in_dim(target_points, offset, block_columns, 1)
        piece_squares = lax.dynamic_slice_in_dim(target_squares, offset, block_columns, 0)
        scores = row_terms[:, None] - pair_distances(source_points, source_squares, target_piece, piece_squares) / entropic_blur
        return -entropic_blur * jax.nn.logsumexp(scores, axis=0)

    offsets = jnp.arange(columns // block_columns, dtype=jnp.int32) * block_columns
    return lax.map(one_block, offsets).reshape(columns)


def mapped_points(source_points, source_squares, target_points, target_squares, column_terms):
    row_count = source_points.shape[1]
    block_rows = math.gcd(row_count, 512)
    groups = NTGT // T_DEV
    target_values = target_points.astype(jnp.float32).reshape(DIM, groups, T_DEV)

    def one_block(offset):
        source_piece = lax.dynamic_slice_in_dim(source_points, offset, block_rows, 1)
        piece_squares = lax.dynamic_slice_in_dim(source_squares, offset, block_rows, 0)
        scores = column_terms[None, :] - pair_distances(source_piece, piece_squares, target_points, target_squares) / entropic_blur
        scores = scores.reshape(block_rows, groups, T_DEV)
        maxima = jnp.max(scores, axis=2)
        weights = jnp.exp(scores - maxima[:, :, None])
        totals = jnp.sum(weights, axis=2)
        rounded = lax.optimization_barrier(weights.astype(jnp.bfloat16)).astype(jnp.float32)
        weighted = jnp.einsum("bgt,dgt->bgd", rounded, target_values, precision=lax.Precision.HIGHEST)
        highest = jnp.max(maxima, axis=1)
        scaling = jnp.exp(maxima - highest[:, None])
        masses = jnp.sum(totals * scaling, axis=1)
        return jnp.sum(weighted * scaling[:, :, None], axis=1) / masses[:, None]

    offsets = jnp.arange(row_count // block_rows, dtype=jnp.int32) * block_rows
    return lax.map(one_block, offsets).reshape(row_count, DIM).T


def reference(source_points, target_points, source_mass, target_mass, target_start):
    source_squares = point_squares(source_points)
    target_squares = point_squares(target_points)
    source_terms = source_mass - math.log(NSRC)
    target_terms = target_mass - math.log(NTGT)
    target_potential = target_start
    source_potential = jnp.zeros_like(source_mass)
    for iteration in range(ITERS):
        source_potential = source_update(source_points, source_squares, target_points, target_squares, target_potential / entropic_blur + target_terms)
        target_potential = target_update(source_points, source_squares, source_potential / entropic_blur + source_terms, target_points, target_squares)
    mapped_cells = mapped_points(source_points, source_squares, target_points, target_squares, target_potential / entropic_blur + target_terms)
    return (source_potential, target_potential, mapped_cells)
```

```python
import functools
import math

import jax
import jax.numpy as jnp
from jax import lax
from jax.experimental import pallas as pl
from jax.experimental.pallas import tpu as pltpu
from jax.sharding import PartitionSpec as P

ITERS = 2
MESH = pl.DeviceIdType.MESH
LOG2E = math.log2(math.e)
LN2 = math.log(2.0)
DEPTH = 128


def split3(value):
    high = value.astype(jnp.bfloat16).astype(jnp.float32)
    rest = value - high
    mid = rest.astype(jnp.bfloat16).astype(jnp.float32)
    return high, mid, rest - mid


def kernel(
    n_src, n_tgt, base,
    x_ref, y_ref, sm_ref, tm_ref, g0_ref,
    f_ref, g_ref, out_ref,
    xa, ya, xsq, ysq, fbuf, gbuf, vals, pieces,
    fsend, frecv, gsend, grecv, vsend, vrecv, osend, orecv,
):
    dim, rows = x_ref.shape
    columns = y_ref.shape[1]
    s = lax.axis_index("src")
    t = lax.axis_index("tgt")
    half = dim // 2
    width = 2 * rows // n_tgt

    barrier = pltpu.get_barrier_semaphore()

    def greet_tgt(d, carry):
        pl.semaphore_signal(
            barrier, inc=1, device_id={"tgt": lax.rem(t + d, n_tgt)}, device_id_type=MESH
        )
        return carry

    def greet_src(d, carry):
        pl.semaphore_signal(
            barrier, inc=1, device_id={"src": lax.rem(s + d, n_src)}, device_id_type=MESH
        )
        return carry

    lax.fori_loop(1, n_tgt, greet_tgt, 0)
    lax.fori_loop(1, n_src, greet_src, 0)

    x = x_ref[...].astype(jnp.float32)
    y = y_ref[...].astype(jnp.float32)
    xsq[...] = jnp.sum(x * x, axis=0, keepdims=True)
    ysq[...] = jnp.sum(y * y, axis=0, keepdims=True)
    for k, part in enumerate(split3(x * (4.0 * LOG2E))):
        xa[k * dim : (k + 1) * dim, :] = part.astype(jnp.bfloat16)
        ya[k * dim : (k + 1) * dim, :] = y_ref[...]
    xa[3 * dim :, :] = jnp.zeros((DEPTH - 3 * dim, rows), jnp.bfloat16)
    ya[3 * dim :, :] = jnp.zeros((DEPTH - 3 * dim, columns), jnp.bfloat16)

    def set_terms(ref, value):
        n = value.shape[1]
        row = lax.broadcasted_iota(jnp.int32, (16, n), 0)
        high, mid, low = split3(value)
        block = jnp.where(row == 0, high, jnp.where(row == 1, mid, jnp.where(row == 2, low, 0.0)))
        ref[3 * dim : 3 * dim + 16, :] = block.astype(jnp.bfloat16)

    def set_ones(ref):
        n = ref.shape[1]
        row = lax.broadcasted_iota(jnp.int32, (16, n), 0)
        ref[3 * dim : 3 * dim + 16, :] = jnp.where(row < 3, 1.0, 0.0).astype(jnp.bfloat16)

    def scores(left, right, offset, chunk):
        return lax.dot_general(
            left[...],
            right[:, pl.ds(offset, chunk)],
            (((0,), (0,)), ((), ())),
            preferred_element_type=jnp.float32,
        )

    def lse_pass(left, right, dst, chunk):
        n = right.shape[1]

        def advance(c, carry):
            offset = pl.multiple_of(c * chunk, chunk)
            block = scores(left, right, offset, chunk)
            top = jnp.max(block, axis=0, keepdims=True)
            total = jnp.sum(jnp.exp2(block - top), axis=0, keepdims=True)
            dst[:, pl.ds(offset, chunk)] = top + jnp.log2(total)
            return carry

        lax.fori_loop(0, n // chunk, advance, 0)

    def send_all(buf, me, axis, count, send, recv):
        def one(d, carry):
            pltpu.make_async_remote_copy(
                src_ref=buf.at[me],
                dst_ref=buf.at[me],
                send_sem=send,
                recv_sem=recv,
                device_id={axis: lax.rem(me + d, count)},
                device_id_type=MESH,
            ).start()
            return carry

        lax.fori_loop(1, count, one, 0)

    def whole(buf, count, axis, me, send, recv):
        part = buf.at[pl.ds(0, count - 1)]
        return pltpu.make_async_remote_copy(
            src_ref=part,
            dst_ref=part,
            send_sem=send,
            recv_sem=recv,
            device_id={axis: lax.rem(me + 1, count)},
            device_id_type=MESH,
        )

    def combine(buf):
        values = buf[...]
        top = jnp.max(values, axis=0)
        return top + jnp.log2(jnp.sum(jnp.exp2(values - top[None]), axis=0))

    column_terms = LOG2E * (2.0 * g0_ref[...] + tm_ref[...] - 2.0 * ysq[...]) - base
    for iteration in range(ITERS):
        set_terms(ya, column_terms)
        set_ones(xa)
        mine = fbuf.at[iteration]
        lse_pass(ya, xa, mine.at[t], 512)
        if iteration == 0:
            pl.semaphore_wait(barrier, n_src + n_tgt - 2)
        send_all(mine, t, "tgt", n_tgt, fsend.at[iteration], frecv.at[iteration])
        whole(mine, n_tgt, "tgt", t, fsend.at[iteration], frecv.at[iteration]).wait_recv()
        row_lse = combine(mine)
        if iteration == ITERS - 1:
            f_ref[...] = xsq[...] - (0.5 * LN2) * row_lse
        set_terms(xa, LOG2E * sm_ref[...] - base - row_lse)
        set_ones(ya)
        mine = gbuf.at[iteration]
        lse_pass(xa, ya, mine.at[s], 256)
        send_all(mine, s, "src", n_src, gsend.at[iteration], grecv.at[iteration])
        whole(mine, n_src, "src", s, gsend.at[iteration], grecv.at[iteration]).wait_recv()
        column_lse = combine(mine)
        if iteration == ITERS - 1:
            g_ref[...] = ysq[...] - (0.5 * LN2) * column_lse
        column_terms = LOG2E * tm_ref[...] - base - column_lse

    set_terms(ya, column_terms)
    set_ones(xa)
    chunk = 512

    def map_rows(c, carry):
        offset = pl.multiple_of(c * chunk, chunk)
        block = scores(ya, xa, offset, chunk)
        top = jnp.max(block, axis=0, keepdims=True)
        weights = jnp.exp2(block - top)
        total = jnp.sum(weights, axis=0, keepdims=True)
        summed = lax.dot_general(
            y_ref[...],
            weights.astype(jnp.bfloat16),
            (((1,), (0,)), ((), ())),
            preferred_element_type=jnp.float32,
        )
        mean = summed / total
        lse = jnp.broadcast_to(top + jnp.log2(total), (8, chunk))
        for h in range(2):
            vals[h, 0:half, pl.ds(offset, chunk)] = mean[h * half : (h + 1) * half]
            vals[h, half : half + 8, pl.ds(offset, chunk)] = lse
        return carry

    lax.fori_loop(0, rows // chunk, map_rows, 0)

    def column_of(p):
        return pl.multiple_of((p // 2) * width, width)

    def send_piece(d, carry):
        p = lax.rem(t + d, n_tgt)
        pltpu.make_async_remote_copy(
            src_ref=vals.at[lax.rem(p, 2), :, pl.ds(column_of(p), width)],
            dst_ref=pieces.at[t],
            send_sem=vsend,
            recv_sem=vrecv,
            device_id={"tgt": p},
            device_id_type=MESH,
        ).start()
        return carry

    lax.fori_loop(1, n_tgt, send_piece, 0)
    pieces[t] = vals[lax.rem(t, 2), :, pl.ds(column_of(t), width)]
    whole(pieces, n_tgt, "tgt", t, vsend, vrecv).wait_recv()
    lse = pieces[:, half : half + 1, :]
    top = jnp.max(lse, axis=0, keepdims=True)
    share = jnp.exp2(lse - top)
    image = jnp.sum(pieces[:, 0:half, :] * share, axis=0) / jnp.sum(share, axis=0)
    spot = (pl.ds(pl.multiple_of(lax.rem(t, 2) * half, half), half), pl.ds(column_of(t), width))
    out_ref[spot] = image

    def send_image(d, carry):
        pltpu.make_async_remote_copy(
            src_ref=out_ref.at[spot],
            dst_ref=out_ref.at[spot],
            send_sem=osend,
            recv_sem=orecv,
            device_id={"tgt": lax.rem(t + d, n_tgt)},
            device_id_type=MESH,
        ).start()
        return carry

    lax.fori_loop(1, n_tgt, send_image, 0)

    def all_images():
        part = pieces.at[pl.ds(0, n_tgt - 1), 0:half, :]
        return pltpu.make_async_remote_copy(
            src_ref=part,
            dst_ref=part,
            send_sem=osend,
            recv_sem=orecv,
            device_id={"tgt": lax.rem(t + 1, n_tgt)},
            device_id_type=MESH,
        )

    all_images().wait_recv()
    for iteration in range(ITERS):
        whole(fbuf.at[iteration], n_tgt, "tgt", t, fsend.at[iteration], frecv.at[iteration]).wait_send()
        whole(gbuf.at[iteration], n_src, "src", s, gsend.at[iteration], grecv.at[iteration]).wait_send()
    whole(pieces, n_tgt, "tgt", t, vsend, vrecv).wait_send()
    all_images().wait_send()


def solution(mesh):
    n_src, n_tgt = mesh.shape["src"], mesh.shape["tgt"]

    def local(source_points, target_points, source_mass, target_mass, target_start):
        dim, rows = source_points.shape
        columns = target_points.shape[1]
        f32 = jnp.float32
        vmem = pl.BlockSpec(memory_space=pltpu.VMEM)
        dma = pltpu.SemaphoreType.DMA
        f, g, mapped = pl.pallas_call(
            functools.partial(kernel, n_src, n_tgt, math.log2(rows * n_src)),
            out_shape=(
                jax.ShapeDtypeStruct((1, rows), f32),
                jax.ShapeDtypeStruct((1, columns), f32),
                jax.ShapeDtypeStruct((dim, rows), f32),
            ),
            in_specs=[vmem] * 5,
            out_specs=(vmem,) * 3,
            scratch_shapes=[
                pltpu.VMEM((DEPTH, rows), jnp.bfloat16),
                pltpu.VMEM((DEPTH, columns), jnp.bfloat16),
                pltpu.VMEM((1, rows), f32),
                pltpu.VMEM((1, columns), f32),
                pltpu.VMEM((ITERS, n_tgt, 1, rows), f32),
                pltpu.VMEM((ITERS, n_src, 1, columns), f32),
                pltpu.VMEM((2, dim // 2 + 8, rows), f32),
                pltpu.VMEM((n_tgt, dim // 2 + 8, 2 * rows // n_tgt), f32),
                dma((ITERS,)),
                dma((ITERS,)),
                dma((ITERS,)),
                dma((ITERS,)),
                dma,
                dma,
                dma,
                dma,
            ],
            compiler_params=pltpu.CompilerParams(
                collective_id=0, has_side_effects=True, vmem_limit_bytes=50 << 20
            ),
        )(
            source_points,
            target_points,
            source_mass.reshape(1, rows),
            target_mass.reshape(1, columns),
            target_start.reshape(1, columns),
        )
        return f.reshape(rows), g.reshape(columns), mapped

    placed = (P(None, "src"), P(None, "tgt"), P("src"), P("tgt"), P("tgt"))
    return jax.shard_map(
        local,
        mesh=mesh,
        in_specs=placed,
        out_specs=(P("src"), P("tgt"), P(None, "src")),
        check_vma=False,
    )
```

```python
import functools
import math

import jax
import jax.numpy as jnp
from jax import lax
from jax.experimental import pallas as pl
from jax.experimental.pallas import tpu as pltpu
from jax.sharding import PartitionSpec as P

ITERS = 2
MESH = pl.DeviceIdType.MESH
LOG2E = math.log2(math.e)
LN2 = math.log(2.0)
DEPTH = 128
CHUNKS = 4
HALVES = 2


def split3(value):
    high = value.astype(jnp.bfloat16).astype(jnp.float32)
    rest = value - high
    mid = rest.astype(jnp.bfloat16).astype(jnp.float32)
    return high, mid, rest - mid


def term_rows(value):
    n = value.shape[1]
    row = lax.broadcasted_iota(jnp.int32, (16, n), 0)
    high, mid, low = split3(value)
    block = jnp.where(row == 0, high, jnp.where(row == 1, mid, jnp.where(row == 2, low, 0.0)))
    return block.astype(jnp.bfloat16)


def one_rows(n):
    row = lax.broadcasted_iota(jnp.int32, (16, n), 0)
    return jnp.where(row < 3, 1.0, 0.0).astype(jnp.bfloat16)


def combine(values):
    top = jnp.max(values, axis=0)
    return top + jnp.log2(jnp.sum(jnp.exp2(values - top[None]), axis=0))


def scores(left, right):
    return lax.dot_general(
        left, right, (((0,), (0,)), ((), ())), preferred_element_type=jnp.float32
    )


def partial(block):
    n = block.shape[1]
    groups = block.reshape(block.shape[0] // 8, 8, n)
    top = jnp.max(groups, axis=0)
    return top, jnp.sum(jnp.exp2(groups - top[None]), axis=0)


def merge(first, second):
    top = jnp.maximum(first[0], second[0])
    return top, first[1] * jnp.exp2(first[0] - top) + second[1] * jnp.exp2(second[0] - top)


def finish(pair):
    top = jnp.max(pair[0], axis=0, keepdims=True)
    return top + jnp.log2(jnp.sum(pair[1] * jnp.exp2(pair[0] - top), axis=0, keepdims=True))


def kernel(
    n_src, n_tgt, src_base, tgt_base,
    x_hbm, y_hbm, sm_hbm, tm_hbm, g0_hbm,
    f_ref, g_ref, out_ref,
    x_ref, y_ref, sm_ref, tm_ref, g0_ref,
    xr, xc, yr, yc, xsq, ysq, rtop, rsum, ctop, csum, fbuf, gbuf, vals, pieces,
    loads, fsend, frecv, gsend, grecv, vsend, vrecv, osend, orecv,
):
    dim, rows = x_ref.shape
    columns = y_ref.shape[1]
    s = lax.axis_index("src")
    t = lax.axis_index("tgt")
    half = dim // 2
    width = 2 * rows // n_tgt
    chunk = rows // CHUNKS
    span = columns // HALVES

    copies = [
        pltpu.make_async_copy(a, b, loads.at[k])
        for k, (a, b) in enumerate(
            (
                (x_hbm, x_ref),
                (y_hbm, y_ref),
                (sm_hbm, sm_ref),
                (tm_hbm, tm_ref),
                (g0_hbm, g0_ref),
            )
        )
    ]
    for copy in copies:
        copy.start()

    barrier = pltpu.get_barrier_semaphore()

    def greet_tgt(d, carry):
        pl.semaphore_signal(
            barrier, inc=1, device_id={"tgt": lax.rem(t + d, n_tgt)}, device_id_type=MESH
        )
        return carry

    def greet_src(d, carry):
        pl.semaphore_signal(
            barrier, inc=1, device_id={"src": lax.rem(s + d, n_src)}, device_id_type=MESH
        )
        return carry

    lax.fori_loop(1, n_tgt, greet_tgt, 0)
    lax.fori_loop(1, n_src, greet_src, 0)
    for copy in copies:
        copy.wait()

    x = x_ref[...].astype(jnp.float32)
    y = y_ref[...].astype(jnp.float32)
    xsq[...] = jnp.sum(x * x, axis=0, keepdims=True)
    ysq[...] = jnp.sum(y * y, axis=0, keepdims=True)
    for k, part in enumerate(split3(x * (4.0 * LOG2E))):
        rounded = part.astype(jnp.bfloat16)
        at = slice(k * dim, (k + 1) * dim)
        xr[at, :] = rounded
        xc[at, :] = rounded
        yr[at, :] = y_ref[...]
        yc[at, :] = y_ref[...]
    used = 3 * dim
    extra = slice(used, used + 16)
    for ref in (xr, xc, yr, yc):
        ref[used:, :] = jnp.zeros((DEPTH - used, ref.shape[1]), jnp.bfloat16)
    xr[extra, :] = one_rows(rows)
    yc[extra, :] = one_rows(columns)

    def send_all(buf, me, axis, count, send, recv):
        def one(d, carry):
            pltpu.make_async_remote_copy(
                src_ref=buf.at[me],
                dst_ref=buf.at[me],
                send_sem=send,
                recv_sem=recv,
                device_id={axis: lax.rem(me + d, count)},
                device_id_type=MESH,
            ).start()
            return carry

        lax.fori_loop(1, count, one, 0)

    def whole(buf, count, axis, me, send, recv):
        part = buf.at[pl.ds(0, count - 1)]
        return pltpu.make_async_remote_copy(
            src_ref=part,
            dst_ref=part,
            send_sem=send,
            recv_sem=recv,
            device_id={axis: lax.rem(me + 1, count)},
            device_id_type=MESH,
        )

    def f_all(i, c):
        return whole(fbuf.at[i, c], n_tgt, "tgt", t, fsend.at[i, c], frecv.at[i, c])

    def g_all(i, h):
        return whole(gbuf.at[i, h], n_src, "src", s, gsend.at[i, h], grecv.at[i, h])

    for iteration in range(ITERS):
        for h in range(HALVES):
            cols = slice(h * span, (h + 1) * span)
            if iteration == 0:
                terms = (
                    LOG2E * (2.0 * g0_ref[:, cols] + tm_ref[:, cols] - 2.0 * ysq[:, cols])
                    - tgt_base
                )
            else:
                g_all(iteration - 1, h).wait_recv()
                terms = LOG2E * tm_ref[:, cols] - tgt_base - combine(gbuf[iteration - 1, h])
            yr[extra, cols] = term_rows(terms)
            for c in range(CHUNKS):
                at = slice(c * chunk, (c + 1) * chunk)
                pair = partial(scores(yr[:, cols], xr[:, at]))
                if h > 0:
                    pair = merge((rtop[:, at], rsum[:, at]), pair)
                if h < HALVES - 1:
                    rtop[:, at], rsum[:, at] = pair
                else:
                    fbuf[iteration, c, t] = finish(pair)
                    if iteration > 0:
                        send_all(
                            fbuf.at[iteration, c], t, "tgt", n_tgt,
                            fsend.at[iteration, c], frecv.at[iteration, c],
                        )
        if iteration == 0:
            pl.semaphore_wait(barrier, n_src + n_tgt - 2)
            for c in range(CHUNKS):
                send_all(
                    fbuf.at[iteration, c], t, "tgt", n_tgt,
                    fsend.at[iteration, c], frecv.at[iteration, c],
                )
        for c in range(CHUNKS):
            at = slice(c * chunk, (c + 1) * chunk)
            f_all(iteration, c).wait_recv()
            row_lse = combine(fbuf[iteration, c])
            if iteration == ITERS - 1:
                f_ref[:, at] = xsq[:, at] - (0.5 * LN2) * row_lse
            xc[extra, at] = term_rows(LOG2E * sm_ref[:, at] - src_base - row_lse)
            for h in range(HALVES):
                cols = slice(h * span, (h + 1) * span)
                pair = partial(scores(xc[:, at], yc[:, cols]))
                if c > 0:
                    pair = merge((ctop[:, cols], csum[:, cols]), pair)
                if c < CHUNKS - 1:
                    ctop[:, cols], csum[:, cols] = pair
                else:
                    gbuf[iteration, h, s] = finish(pair)
                    send_all(
                        gbuf.at[iteration, h], s, "src", n_src,
                        gsend.at[iteration, h], grecv.at[iteration, h],
                    )

    for h in range(HALVES):
        cols = slice(h * span, (h + 1) * span)
        g_all(ITERS - 1, h).wait_recv()
        column_lse = combine(gbuf[ITERS - 1, h])
        g_ref[:, cols] = ysq[:, cols] - (0.5 * LN2) * column_lse
        yr[extra, cols] = term_rows(LOG2E * tm_ref[:, cols] - tgt_base - column_lse)

    def send_piece(d, first):
        p = first + d

        @pl.when(p != t)
        def _():
            pltpu.make_async_remote_copy(
                src_ref=vals.at[lax.rem(p, 2), :, pl.ds(column_of(p), width)],
                dst_ref=pieces.at[t],
                send_sem=vsend,
                recv_sem=vrecv,
                device_id={"tgt": p},
                device_id_type=MESH,
            ).start()

        return first

    def column_of(p):
        return pl.multiple_of((p // 2) * width, width)

    owners = n_tgt // CHUNKS
    for turn in (2, 1, 3, 0):
        c = lax.rem(t // owners + turn, CHUNKS)
        at = pl.ds(pl.multiple_of(c * chunk, chunk), chunk)
        block = scores(yr[...], xr[:, at])
        top = jnp.max(block, axis=0, keepdims=True)
        weights = jnp.exp2(block - top)
        total = jnp.sum(weights, axis=0, keepdims=True)
        summed = lax.dot_general(
            y_ref[...],
            weights.astype(jnp.bfloat16),
            (((1,), (0,)), ((), ())),
            preferred_element_type=jnp.float32,
        )
        mean = summed / total
        lse = jnp.broadcast_to(top + jnp.log2(total), (8, chunk))
        for k in range(2):
            vals[k, 0:half, at] = mean[k * half : (k + 1) * half]
            vals[k, half : half + 8, at] = lse
        lax.fori_loop(0, owners, send_piece, c * owners)

    pieces[t] = vals[lax.rem(t, 2), :, pl.ds(column_of(t), width)]
    whole(pieces, n_tgt, "tgt", t, vsend, vrecv).wait_recv()
    lse = pieces[:, half : half + 1, :]
    top = jnp.max(lse, axis=0, keepdims=True)
    share = jnp.exp2(lse - top)
    image = jnp.sum(pieces[:, 0:half, :] * share, axis=0) / jnp.sum(share, axis=0)
    spot = (pl.ds(pl.multiple_of(lax.rem(t, 2) * half, half), half), pl.ds(column_of(t), width))
    out_ref[spot] = image

    def send_image(d, carry):
        pltpu.make_async_remote_copy(
            src_ref=out_ref.at[spot],
            dst_ref=out_ref.at[spot],
            send_sem=osend,
            recv_sem=orecv,
            device_id={"tgt": lax.rem(t + d, n_tgt)},
            device_id_type=MESH,
        ).start()
        return carry

    lax.fori_loop(1, n_tgt, send_image, 0)

    def all_images():
        part = pieces.at[pl.ds(0, n_tgt - 1), 0:half, :]
        return pltpu.make_async_remote_copy(
            src_ref=part,
            dst_ref=part,
            send_sem=osend,
            recv_sem=orecv,
            device_id={"tgt": lax.rem(t + 1, n_tgt)},
            device_id_type=MESH,
        )

    for iteration in range(ITERS):
        for c in range(CHUNKS):
            f_all(iteration, c).wait_send()
        for h in range(HALVES):
            g_all(iteration, h).wait_send()
    whole(pieces, n_tgt, "tgt", t, vsend, vrecv).wait_send()
    all_images().wait_recv()
    all_images().wait_send()


def store(f_in, g_in, out_in, f_out, g_out, out_out, sems):
    copies = [
        pltpu.make_async_copy(a, b, sems.at[k])
        for k, (a, b) in enumerate(((out_in, out_out), (f_in, f_out), (g_in, g_out)))
    ]
    for copy in copies:
        copy.start()
    for copy in copies:
        copy.wait()


def solution(mesh):
    n_src, n_tgt = mesh.shape["src"], mesh.shape["tgt"]

    def local(source_points, target_points, source_mass, target_mass, target_start):
        dim, rows = source_points.shape
        columns = target_points.shape[1]
        f32, bf16 = jnp.float32, jnp.bfloat16
        vmem = pl.BlockSpec(memory_space=pltpu.VMEM)
        hbm = pl.BlockSpec(memory_space=pltpu.HBM)
        dma = pltpu.SemaphoreType.DMA
        outs = (
            jax.ShapeDtypeStruct((1, rows), f32),
            jax.ShapeDtypeStruct((1, columns), f32),
            jax.ShapeDtypeStruct((dim, rows), f32),
        )
        chunk, span = rows // CHUNKS, columns // HALVES
        results = pl.pallas_call(
            functools.partial(
                kernel, n_src, n_tgt, math.log2(rows * n_src), math.log2(columns * n_tgt)
            ),
            out_shape=outs,
            in_specs=[hbm] * 5,
            out_specs=(vmem,) * 3,
            scratch_shapes=[
                pltpu.VMEM((dim, rows), bf16),
                pltpu.VMEM((dim, columns), bf16),
                pltpu.VMEM((1, rows), f32),
                pltpu.VMEM((1, columns), f32),
                pltpu.VMEM((1, columns), f32),
                pltpu.VMEM((DEPTH, rows), bf16),
                pltpu.VMEM((DEPTH, rows), bf16),
                pltpu.VMEM((DEPTH, columns), bf16),
                pltpu.VMEM((DEPTH, columns), bf16),
                pltpu.VMEM((1, rows), f32),
                pltpu.VMEM((1, columns), f32),
                pltpu.VMEM((8, rows), f32),
                pltpu.VMEM((8, rows), f32),
                pltpu.VMEM((8, columns), f32),
                pltpu.VMEM((8, columns), f32),
                pltpu.VMEM((ITERS, CHUNKS, n_tgt, 1, chunk), f32),
                pltpu.VMEM((ITERS, HALVES, n_src, 1, span), f32),
                pltpu.VMEM((2, dim // 2 + 8, rows), f32),
                pltpu.VMEM((n_tgt, dim // 2 + 8, 2 * rows // n_tgt), f32),
                dma((5,)),
                dma((ITERS, CHUNKS)),
                dma((ITERS, CHUNKS)),
                dma((ITERS, HALVES)),
                dma((ITERS, HALVES)),
                dma,
                dma,
                dma,
                dma,
            ],
            compiler_params=pltpu.CompilerParams(
                collective_id=0, has_side_effects=True, vmem_limit_bytes=48 << 20
            ),
        )(
            *[pltpu.with_memory_space_constraint(v, pltpu.HBM) for v in (source_points, target_points, source_mass.reshape(1, rows), target_mass.reshape(1, columns), target_start.reshape(1, columns))]
        )
        f, g, mapped = pl.pallas_call(
            store,
            out_shape=outs,
            in_specs=[vmem] * 3,
            out_specs=(hbm,) * 3,
            scratch_shapes=[dma((3,))],
            compiler_params=pltpu.CompilerParams(vmem_limit_bytes=1 << 20),
        )(*results)
        return f.reshape(rows), g.reshape(columns), mapped

    placed = (P(None, "src"), P(None, "tgt"), P("src"), P("tgt"), P("tgt"))
    return jax.shard_map(
        local,
        mesh=mesh,
        in_specs=placed,
        out_specs=(P("src"), P("tgt"), P(None, "src")),
        check_vma=False,
    )
```

```python
import functools
import math

import jax
import jax.numpy as jnp
from jax import lax
from jax.experimental import pallas as pl
from jax.experimental.pallas import tpu as pltpu
from jax.sharding import PartitionSpec as P

ITERS = 2
MESH = pl.DeviceIdType.MESH
LOG2E = math.log2(math.e)
LN2 = math.log(2.0)
DEPTH = 128
CHUNKS = 4
HALVES = 1
PHASES = 2


def far_first(n):
    return sorted(range(n), key=lambda d: -min(d, n - d))


def split3(value):
    high = value.astype(jnp.bfloat16).astype(jnp.float32)
    rest = value - high
    mid = rest.astype(jnp.bfloat16).astype(jnp.float32)
    return high, mid, rest - mid


def term_rows(value):
    n = value.shape[1]
    row = lax.broadcasted_iota(jnp.int32, (16, n), 0)
    high, mid, low = split3(value)
    block = jnp.where(row == 0, high, jnp.where(row == 1, mid, jnp.where(row == 2, low, 0.0)))
    return block.astype(jnp.bfloat16)


def one_rows(n):
    row = lax.broadcasted_iota(jnp.int32, (16, n), 0)
    return jnp.where(row < 3, 1.0, 0.0).astype(jnp.bfloat16)


def combine(values):
    top = jnp.max(values, axis=0)
    return top + jnp.log2(jnp.sum(jnp.exp2(values - top[None]), axis=0))


def scores(left, right):
    return lax.dot_general(
        left, right, (((0,), (0,)), ((), ())), preferred_element_type=jnp.float32
    )


def partial(block):
    n = block.shape[1]
    groups = block.reshape(block.shape[0] // 8, 8, n)
    top = jnp.max(groups, axis=0)
    return top, jnp.sum(jnp.exp2(groups - top[None]), axis=0)


def merge(first, second):
    top = jnp.maximum(first[0], second[0])
    return top, first[1] * jnp.exp2(first[0] - top) + second[1] * jnp.exp2(second[0] - top)


def finish(pair):
    top = jnp.max(pair[0], axis=0, keepdims=True)
    return top + jnp.log2(jnp.sum(pair[1] * jnp.exp2(pair[0] - top), axis=0, keepdims=True))


def kernel(
    n_src, n_tgt, src_base, tgt_base,
    x_hbm, y_hbm, sm_hbm, tm_hbm, g0_hbm,
    f_ref, g_ref, out_ref,
    x_ref, y_ref, sm_ref, tm_ref, g0_ref,
    xr, xc, yr, yc, xsq, ysq, rtop, rsum, ctop, csum, fbuf, gbuf, vals, logs, pieces, shares,
    loads, fsend, frecv, gsend, grecv, vsend, vrecv, lsend, lrecv, osend, orecv,
):
    dim, rows = x_ref.shape
    columns = y_ref.shape[1]
    s = lax.axis_index("src")
    t = lax.axis_index("tgt")
    groups = dim // 8
    width = groups * rows // (PHASES * n_tgt)
    chunk = rows // CHUNKS
    span = columns // HALVES

    copies = [
        pltpu.make_async_copy(a, b, loads.at[k])
        for k, (a, b) in enumerate(
            (
                (x_hbm, x_ref),
                (y_hbm, y_ref),
                (sm_hbm, sm_ref),
                (tm_hbm, tm_ref),
                (g0_hbm, g0_ref),
            )
        )
    ]
    for copy in copies:
        copy.start()

    nx, ny, nz = 4, n_tgt // 4, n_src // 2
    xs = [lax.rem(t // ny + d, nx) * ny for d in far_first(nx)]
    ys = [lax.rem(lax.rem(t, ny) + d, ny) for d in far_first(ny)]
    zs = [lax.rem(s // 2 + d, nz) * 2 for d in far_first(nz)]
    cs = [1 - lax.rem(s, 2), lax.rem(s, 2)]
    tgt_peers = [b + a for a in ys for b in xs][:-1]
    src_peers = [b + a for b in zs for a in cs][:-1]

    barrier = pltpu.get_barrier_semaphore()
    for axis, peers in (("tgt", tgt_peers), ("src", src_peers)):
        for peer in peers:
            pl.semaphore_signal(barrier, inc=1, device_id={axis: peer}, device_id_type=MESH)
    for copy in copies:
        copy.wait()

    x = x_ref[...].astype(jnp.float32)
    y = y_ref[...].astype(jnp.float32)
    xsq[...] = jnp.sum(x * x, axis=0, keepdims=True)
    ysq[...] = jnp.sum(y * y, axis=0, keepdims=True)
    for k, part in enumerate(split3(x * (4.0 * LOG2E))):
        rounded = part.astype(jnp.bfloat16)
        at = slice(k * dim, (k + 1) * dim)
        xr[at, :] = rounded
        xc[at, :] = rounded
        yr[at, :] = y_ref[...]
        yc[at, :] = y_ref[...]
    used = 3 * dim
    extra = slice(used, used + 16)
    for ref in (xr, xc, yr, yc):
        ref[used:, :] = jnp.zeros((DEPTH - used, ref.shape[1]), jnp.bfloat16)
    xr[extra, :] = one_rows(rows)
    yc[extra, :] = one_rows(columns)

    def send_all(buf, me, axis, count, send, recv):
        for peer in tgt_peers if axis == "tgt" else src_peers:
            pltpu.make_async_remote_copy(
                src_ref=buf.at[me],
                dst_ref=buf.at[me],
                send_sem=send,
                recv_sem=recv,
                device_id={axis: peer},
                device_id_type=MESH,
            ).start()

    def whole(buf, count, axis, me, send, recv):
        part = buf.at[pl.ds(0, count - 1)]
        return pltpu.make_async_remote_copy(
            src_ref=part,
            dst_ref=part,
            send_sem=send,
            recv_sem=recv,
            device_id={axis: lax.rem(me + 1, count)},
            device_id_type=MESH,
        )

    def f_all(i, c):
        return whole(fbuf.at[i, c], n_tgt, "tgt", t, fsend.at[i, c], frecv.at[i, c])

    def g_all(i, h):
        return whole(gbuf.at[i, h], n_src, "src", s, gsend.at[i, h], grecv.at[i, h])

    for iteration in range(ITERS):
        for h in range(HALVES):
            cols = slice(h * span, (h + 1) * span)
            if iteration == 0:
                terms = (
                    LOG2E * (2.0 * g0_ref[:, cols] + tm_ref[:, cols] - 2.0 * ysq[:, cols])
                    - tgt_base
                )
            else:
                g_all(iteration - 1, h).wait_recv()
                terms = LOG2E * tm_ref[:, cols] - tgt_base - combine(gbuf[iteration - 1, h])
            yr[extra, cols] = term_rows(terms)
            for c in range(CHUNKS):
                at = slice(c * chunk, (c + 1) * chunk)
                pair = partial(scores(yr[:, cols], xr[:, at]))
                if h > 0:
                    pair = merge((rtop[:, at], rsum[:, at]), pair)
                if h < HALVES - 1:
                    rtop[:, at], rsum[:, at] = pair
                else:
                    fbuf[iteration, c, t] = finish(pair)
                    if iteration > 0:
                        send_all(
                            fbuf.at[iteration, c], t, "tgt", n_tgt,
                            fsend.at[iteration, c], frecv.at[iteration, c],
                        )
        if iteration == 0:
            pl.semaphore_wait(barrier, n_src + n_tgt - 2)
            for c in range(CHUNKS):
                send_all(
                    fbuf.at[iteration, c], t, "tgt", n_tgt,
                    fsend.at[iteration, c], frecv.at[iteration, c],
                )
        for c in range(CHUNKS):
            at = slice(c * chunk, (c + 1) * chunk)
            f_all(iteration, c).wait_recv()
            row_lse = combine(fbuf[iteration, c])
            if iteration == ITERS - 1:
                f_ref[:, at] = xsq[:, at] - (0.5 * LN2) * row_lse
            xc[extra, at] = term_rows(LOG2E * sm_ref[:, at] - src_base - row_lse)
            for h in range(HALVES):
                cols = slice(h * span, (h + 1) * span)
                pair = partial(scores(xc[:, at], yc[:, cols]))
                if c > 0:
                    pair = merge((ctop[:, cols], csum[:, cols]), pair)
                if c < CHUNKS - 1:
                    ctop[:, cols], csum[:, cols] = pair
                else:
                    gbuf[iteration, h, s] = finish(pair)
                    send_all(
                        gbuf.at[iteration, h], s, "src", n_src,
                        gsend.at[iteration, h], grecv.at[iteration, h],
                    )

    for h in range(HALVES):
        cols = slice(h * span, (h + 1) * span)
        g_all(ITERS - 1, h).wait_recv()
        column_lse = combine(gbuf[ITERS - 1, h])
        g_ref[:, cols] = ysq[:, cols] - (0.5 * LN2) * column_lse
        yr[extra, cols] = term_rows(LOG2E * tm_ref[:, cols] - tgt_base - column_lse)

    def place(phase, p):
        return pl.multiple_of(phase * (rows // PHASES) + p // groups * width, width)

    for phase in range(PHASES):
        for turn in range(2):
            k = lax.rem(t // (n_tgt // 2) + 1 + turn, 2)
            at = pl.ds(pl.multiple_of((2 * phase + k) * chunk, chunk), chunk)
            block = scores(yr[...], xr[:, at])
            top = jnp.max(block, axis=0, keepdims=True)
            weights = jnp.exp2(block - top)
            total = jnp.sum(weights, axis=0, keepdims=True)
            summed = lax.dot_general(
                y_ref[...],
                weights.astype(jnp.bfloat16),
                (((1,), (0,)), ((), ())),
                preferred_element_type=jnp.float32,
            )
            mean = summed / total
            for q in range(groups):
                vals[q, :, at] = mean[q * 8 : (q + 1) * 8]
            logs[:, at] = top + jnp.log2(total)
            near = [2 * ny * k + ny * r for r in (1 - lax.rem(t // ny, 2), lax.rem(t // ny, 2))]
            owners = [b + a for a in ys for b in near]
            for p in owners[:-1] if turn == 1 else owners:
                lanes = pl.ds(place(phase, p), width)
                for source, target, send, recv in (
                    (vals.at[lax.rem(p, groups), :, lanes], pieces, vsend, vrecv),
                    (logs.at[:, lanes], shares, lsend, lrecv),
                ):
                    pltpu.make_async_remote_copy(
                        src_ref=source,
                        dst_ref=target.at[phase, t],
                        send_sem=send.at[phase],
                        recv_sem=recv.at[phase],
                        device_id={"tgt": p},
                        device_id_type=MESH,
                    ).start()

    def all_pieces(phase, ref, send, recv):
        part = ref.at[phase, pl.ds(0, n_tgt - 1)]
        return pltpu.make_async_remote_copy(
            src_ref=part,
            dst_ref=part,
            send_sem=send.at[phase],
            recv_sem=recv.at[phase],
            device_id={"tgt": tgt_peers[0]},
            device_id_type=MESH,
        )

    for phase in range(PHASES):
        pieces[phase, t] = vals[lax.rem(t, groups), :, pl.ds(place(phase, t), width)]
        shares[phase, t] = logs[:, pl.ds(place(phase, t), width)]
        all_pieces(phase, shares, lsend, lrecv).wait_recv()
        lse = shares[phase]
        top = jnp.max(lse, axis=0, keepdims=True)
        share = jnp.exp2(lse - top)
        share = share / jnp.sum(share, axis=0, keepdims=True)
        all_pieces(phase, pieces, vsend, vrecv).wait_recv()
        image = jnp.sum(pieces[phase] * share, axis=0)
        spot = (pl.ds(pl.multiple_of(lax.rem(t, groups) * 8, 8), 8), pl.ds(place(phase, t), width))
        out_ref[spot] = image
        for peer in tgt_peers:
            pltpu.make_async_remote_copy(
                src_ref=out_ref.at[spot],
                dst_ref=out_ref.at[spot],
                send_sem=osend.at[phase],
                recv_sem=orecv.at[phase],
                device_id={"tgt": peer},
                device_id_type=MESH,
            ).start()

    for iteration in range(ITERS):
        for c in range(CHUNKS):
            f_all(iteration, c).wait_send()
        for h in range(HALVES):
            g_all(iteration, h).wait_send()
    for phase in range(PHASES):
        all_pieces(phase, shares, lsend, lrecv).wait_send()
        all_pieces(phase, pieces, vsend, vrecv).wait_send()
        all_pieces(phase, pieces, osend, orecv).wait_recv()
        all_pieces(phase, pieces, osend, orecv).wait_send()


def store(f_in, g_in, out_in, f_out, g_out, out_out, sems):
    copies = [
        pltpu.make_async_copy(a, b, sems.at[k])
        for k, (a, b) in enumerate(((out_in, out_out), (f_in, f_out), (g_in, g_out)))
    ]
    for copy in copies:
        copy.start()
    for copy in copies:
        copy.wait()


def solution(mesh):
    n_src, n_tgt = mesh.shape["src"], mesh.shape["tgt"]

    def local(source_points, target_points, source_mass, target_mass, target_start):
        dim, rows = source_points.shape
        columns = target_points.shape[1]
        f32, bf16 = jnp.float32, jnp.bfloat16
        vmem = pl.BlockSpec(memory_space=pltpu.VMEM)
        hbm = pl.BlockSpec(memory_space=pltpu.HBM)
        dma = pltpu.SemaphoreType.DMA
        outs = (
            jax.ShapeDtypeStruct((1, rows), f32),
            jax.ShapeDtypeStruct((1, columns), f32),
            jax.ShapeDtypeStruct((dim, rows), f32),
        )
        chunk, span = rows // CHUNKS, columns // HALVES
        results = pl.pallas_call(
            functools.partial(
                kernel, n_src, n_tgt, math.log2(rows * n_src), math.log2(columns * n_tgt)
            ),
            out_shape=outs,
            in_specs=[hbm] * 5,
            out_specs=(vmem,) * 3,
            scratch_shapes=[
                pltpu.VMEM((dim, rows), bf16),
                pltpu.VMEM((dim, columns), bf16),
                pltpu.VMEM((1, rows), f32),
                pltpu.VMEM((1, columns), f32),
                pltpu.VMEM((1, columns), f32),
                pltpu.VMEM((DEPTH, rows), bf16),
                pltpu.VMEM((DEPTH, rows), bf16),
                pltpu.VMEM((DEPTH, columns), bf16),
                pltpu.VMEM((DEPTH, columns), bf16),
                pltpu.VMEM((1, rows), f32),
                pltpu.VMEM((1, columns), f32),
                pltpu.VMEM((8, rows), f32),
                pltpu.VMEM((8, rows), f32),
                pltpu.VMEM((8, columns), f32),
                pltpu.VMEM((8, columns), f32),
                pltpu.VMEM((ITERS, CHUNKS, n_tgt, 1, chunk), f32),
                pltpu.VMEM((ITERS, HALVES, n_src, 1, span), f32),
                pltpu.VMEM((dim // 8, 8, rows), f32),
                pltpu.VMEM((1, rows), f32),
                pltpu.VMEM((PHASES, n_tgt, 8, dim // 8 * rows // (PHASES * n_tgt)), f32),
                pltpu.VMEM((PHASES, n_tgt, 1, dim // 8 * rows // (PHASES * n_tgt)), f32),
                dma((5,)),
                dma((ITERS, CHUNKS)),
                dma((ITERS, CHUNKS)),
                dma((ITERS, HALVES)),
                dma((ITERS, HALVES)),
                dma((PHASES,)),
                dma((PHASES,)),
                dma((PHASES,)),
                dma((PHASES,)),
                dma((PHASES,)),
                dma((PHASES,)),
            ],
            compiler_params=pltpu.CompilerParams(
                collective_id=0, has_side_effects=True, vmem_limit_bytes=48 << 20
            ),
        )(
            *[pltpu.with_memory_space_constraint(v, pltpu.HBM) for v in (source_points, target_points, source_mass.reshape(1, rows), target_mass.reshape(1, columns), target_start.reshape(1, columns))]
        )
        f, g, mapped = pl.pallas_call(
            store,
            out_shape=outs,
            in_specs=[vmem] * 3,
            out_specs=(hbm,) * 3,
            scratch_shapes=[dma((3,))],
            compiler_params=pltpu.CompilerParams(vmem_limit_bytes=1 << 20),
        )(*results)
        return f.reshape(rows), g.reshape(columns), mapped

    placed = (P(None, "src"), P(None, "tgt"), P("src"), P("tgt"), P("tgt"))
    return jax.shard_map(
        local,
        mesh=mesh,
        in_specs=placed,
        out_specs=(P("src"), P("tgt"), P(None, "src")),
        check_vma=False,
    )
```

```python
import functools
import math

import jax
import jax.numpy as jnp
from jax import lax
from jax.experimental import pallas as pl
from jax.experimental.pallas import tpu as pltpu
from jax.sharding import PartitionSpec as P

ITERS = 2
MESH = pl.DeviceIdType.MESH
LOG2E = math.log2(math.e)
LN2 = math.log(2.0)
DEPTH = 128
CHUNKS = 2
HALVES = 1
PHASES = 2
MAPS = 4
TILE = 256


def far_first(n):
    return sorted(range(n), key=lambda d: -min(d, n - d))


def split3(value):
    high = value.astype(jnp.bfloat16).astype(jnp.float32)
    rest = value - high
    mid = rest.astype(jnp.bfloat16).astype(jnp.float32)
    return high, mid, rest - mid


def term_rows(value):
    n = value.shape[1]
    row = lax.broadcasted_iota(jnp.int32, (16, n), 0)
    high, mid, low = split3(value)
    block = jnp.where(row == 0, high, jnp.where(row == 1, mid, jnp.where(row == 2, low, 0.0)))
    return block.astype(jnp.bfloat16)


def one_rows(n):
    row = lax.broadcasted_iota(jnp.int32, (16, n), 0)
    return jnp.where(row < 3, 1.0, 0.0).astype(jnp.bfloat16)


def combine(values):
    top = jnp.max(values, axis=0)
    return top + jnp.log2(jnp.sum(jnp.exp2(values - top[None]), axis=0))


def scores(left, right):
    return lax.dot_general(
        left, right, (((0,), (0,)), ((), ())), preferred_element_type=jnp.float32
    )


def partial(block):
    n = block.shape[1]
    groups = block.reshape(block.shape[0] // 8, 8, n)
    top = jnp.max(groups, axis=0)
    return top, jnp.sum(jnp.exp2(groups - top[None]), axis=0)


def tiled(left, right, kept, reduced):
    tops, sums = [], []
    for a in range(kept.start, kept.stop, TILE):
        pair = None
        for b in range(reduced.start, reduced.stop, TILE):
            piece = partial(scores(left[:, b : b + TILE], right[:, a : a + TILE]))
            pair = piece if pair is None else merge(pair, piece)
        tops.append(pair[0])
        sums.append(pair[1])
    return jnp.concatenate(tops, axis=1), jnp.concatenate(sums, axis=1)


def merge(first, second):
    top = jnp.maximum(first[0], second[0])
    return top, first[1] * jnp.exp2(first[0] - top) + second[1] * jnp.exp2(second[0] - top)


def finish(pair):
    top = jnp.max(pair[0], axis=0, keepdims=True)
    return top + jnp.log2(jnp.sum(pair[1] * jnp.exp2(pair[0] - top), axis=0, keepdims=True))


def kernel(
    n_src, n_tgt, src_base, tgt_base,
    x_hbm, y_hbm, sm_hbm, tm_hbm, g0_hbm,
    f_ref, g_ref, out_ref,
    x_ref, y_ref, sm_ref, tm_ref, g0_ref,
    xr, xc, yr, yc, xsq, ysq, rtop, rsum, ctop, csum, fbuf, gbuf, vals, logs, pieces, shares,
    loads, fsend, frecv, gsend, grecv, vsend, vrecv, lsend, lrecv, osend, orecv,
):
    dim, rows = x_ref.shape
    columns = y_ref.shape[1]
    s = lax.axis_index("src")
    t = lax.axis_index("tgt")
    groups = dim // 8
    width = groups * rows // (PHASES * n_tgt)
    chunk = rows // CHUNKS
    span = columns // HALVES

    copies = [
        pltpu.make_async_copy(a, b, loads.at[k])
        for k, (a, b) in enumerate(
            (
                (x_hbm, x_ref),
                (y_hbm, y_ref),
                (sm_hbm, sm_ref),
                (tm_hbm, tm_ref),
                (g0_hbm, g0_ref),
            )
        )
    ]
    for copy in copies:
        copy.start()

    nx, ny, nz = 4, n_tgt // 4, n_src // 2
    xs = [lax.rem(t // ny + d, nx) * ny for d in far_first(nx)]
    ys = [lax.rem(lax.rem(t, ny) + d, ny) for d in far_first(ny)]
    zs = [lax.rem(s // 2 + d, nz) * 2 for d in far_first(nz)]
    cs = [1 - lax.rem(s, 2), lax.rem(s, 2)]
    tgt_peers = [b + a for a in ys for b in xs][:-1]
    src_peers = [b + a for b in zs for a in cs][:-1]

    barrier = pltpu.get_barrier_semaphore()
    for axis, peers in (("tgt", tgt_peers), ("src", src_peers)):
        for peer in peers:
            pl.semaphore_signal(barrier, inc=1, device_id={axis: peer}, device_id_type=MESH)
    for copy in copies:
        copy.wait()

    x = x_ref[...].astype(jnp.float32)
    y = y_ref[...].astype(jnp.float32)
    xsq[...] = jnp.sum(x * x, axis=0, keepdims=True)
    ysq[...] = jnp.sum(y * y, axis=0, keepdims=True)
    for k, part in enumerate(split3(x * (4.0 * LOG2E))):
        rounded = part.astype(jnp.bfloat16)
        at = slice(k * dim, (k + 1) * dim)
        xr[at, :] = rounded
        xc[at, :] = rounded
        yr[at, :] = y_ref[...]
        yc[at, :] = y_ref[...]
    used = 3 * dim
    extra = slice(used, used + 16)
    for ref in (xr, xc, yr, yc):
        ref[used:, :] = jnp.zeros((DEPTH - used, ref.shape[1]), jnp.bfloat16)
    xr[extra, :] = one_rows(rows)
    yc[extra, :] = one_rows(columns)

    def send_all(buf, me, axis, count, send, recv):
        for peer in tgt_peers if axis == "tgt" else src_peers:
            pltpu.make_async_remote_copy(
                src_ref=buf.at[me],
                dst_ref=buf.at[me],
                send_sem=send,
                recv_sem=recv,
                device_id={axis: peer},
                device_id_type=MESH,
            ).start()

    def whole(buf, count, axis, me, send, recv):
        part = buf.at[pl.ds(0, count - 1)]
        return pltpu.make_async_remote_copy(
            src_ref=part,
            dst_ref=part,
            send_sem=send,
            recv_sem=recv,
            device_id={axis: lax.rem(me + 1, count)},
            device_id_type=MESH,
        )

    def f_all(i, c):
        return whole(fbuf.at[i, c], n_tgt, "tgt", t, fsend.at[i, c], frecv.at[i, c])

    def g_all(i, h):
        return whole(gbuf.at[i, h], n_src, "src", s, gsend.at[i, h], grecv.at[i, h])

    for iteration in range(ITERS):
        for h in range(HALVES):
            cols = slice(h * span, (h + 1) * span)
            if iteration == 0:
                terms = (
                    LOG2E * (2.0 * g0_ref[:, cols] + tm_ref[:, cols] - 2.0 * ysq[:, cols])
                    - tgt_base
                )
            else:
                g_all(iteration - 1, h).wait_recv()
                terms = LOG2E * tm_ref[:, cols] - tgt_base - combine(gbuf[iteration - 1, h])
            yr[extra, cols] = term_rows(terms)
            for c in range(CHUNKS):
                at = slice(c * chunk, (c + 1) * chunk)
                pair = tiled(yr, xr, at, cols)
                if h > 0:
                    pair = merge((rtop[:, at], rsum[:, at]), pair)
                if h < HALVES - 1:
                    rtop[:, at], rsum[:, at] = pair
                else:
                    fbuf[iteration, c, t] = finish(pair)
                    if iteration > 0:
                        send_all(
                            fbuf.at[iteration, c], t, "tgt", n_tgt,
                            fsend.at[iteration, c], frecv.at[iteration, c],
                        )
        if iteration == 0:
            pl.semaphore_wait(barrier, n_src + n_tgt - 2)
            for c in range(CHUNKS):
                send_all(
                    fbuf.at[iteration, c], t, "tgt", n_tgt,
                    fsend.at[iteration, c], frecv.at[iteration, c],
                )
        for c in range(CHUNKS):
            at = slice(c * chunk, (c + 1) * chunk)
            f_all(iteration, c).wait_recv()
            row_lse = combine(fbuf[iteration, c])
            if iteration == ITERS - 1:
                f_ref[:, at] = xsq[:, at] - (0.5 * LN2) * row_lse
            xc[extra, at] = term_rows(LOG2E * sm_ref[:, at] - src_base - row_lse)
            for h in range(HALVES):
                cols = slice(h * span, (h + 1) * span)
                pair = tiled(xc, yc, cols, at)
                if c > 0:
                    pair = merge((ctop[:, cols], csum[:, cols]), pair)
                if c < CHUNKS - 1:
                    ctop[:, cols], csum[:, cols] = pair
                else:
                    gbuf[iteration, h, s] = finish(pair)
                    send_all(
                        gbuf.at[iteration, h], s, "src", n_src,
                        gsend.at[iteration, h], grecv.at[iteration, h],
                    )

    for h in range(HALVES):
        cols = slice(h * span, (h + 1) * span)
        g_all(ITERS - 1, h).wait_recv()
        column_lse = combine(gbuf[ITERS - 1, h])
        g_ref[:, cols] = ysq[:, cols] - (0.5 * LN2) * column_lse
        yr[extra, cols] = term_rows(LOG2E * tm_ref[:, cols] - tgt_base - column_lse)

    def place(phase, p):
        return pl.multiple_of(phase * (rows // PHASES) + p // groups * width, width)

    piece = rows // MAPS
    for phase in range(PHASES):
        for turn in range(2):
            k = lax.rem(t // (n_tgt // 2) + 1 + turn, 2)
            at = pl.ds(pl.multiple_of((2 * phase + k) * piece, piece), piece)
            block = scores(yr[...], xr[:, at])
            top = jnp.max(block, axis=0, keepdims=True)
            weights = jnp.exp2(block - top)
            total = jnp.sum(weights, axis=0, keepdims=True)
            summed = lax.dot_general(
                y_ref[...],
                weights.astype(jnp.bfloat16),
                (((1,), (0,)), ((), ())),
                preferred_element_type=jnp.float32,
            )
            mean = summed / total
            for q in range(groups):
                vals[q, :, at] = mean[q * 8 : (q + 1) * 8]
            logs[:, at] = top + jnp.log2(total)
            near = [2 * ny * k + ny * r for r in (1 - lax.rem(t // ny, 2), lax.rem(t // ny, 2))]
            owners = [b + a for a in ys for b in near]
            for p in owners[:-1] if turn == 1 else owners:
                lanes = pl.ds(place(phase, p), width)
                for source, target, send, recv in (
                    (vals.at[lax.rem(p, groups), :, lanes], pieces, vsend, vrecv),
                    (logs.at[:, lanes], shares, lsend, lrecv),
                ):
                    pltpu.make_async_remote_copy(
                        src_ref=source,
                        dst_ref=target.at[phase, t],
                        send_sem=send.at[phase],
                        recv_sem=recv.at[phase],
                        device_id={"tgt": p},
                        device_id_type=MESH,
                    ).start()

    def all_pieces(phase, ref, send, recv):
        part = ref.at[phase, pl.ds(0, n_tgt - 1)]
        return pltpu.make_async_remote_copy(
            src_ref=part,
            dst_ref=part,
            send_sem=send.at[phase],
            recv_sem=recv.at[phase],
            device_id={"tgt": tgt_peers[0]},
            device_id_type=MESH,
        )

    for phase in range(PHASES):
        pieces[phase, t] = vals[lax.rem(t, groups), :, pl.ds(place(phase, t), width)]
        shares[phase, t] = logs[:, pl.ds(place(phase, t), width)]
        all_pieces(phase, shares, lsend, lrecv).wait_recv()
        lse = shares[phase]
        top = jnp.max(lse, axis=0, keepdims=True)
        share = jnp.exp2(lse - top)
        share = share / jnp.sum(share, axis=0, keepdims=True)
        all_pieces(phase, pieces, vsend, vrecv).wait_recv()
        image = jnp.sum(pieces[phase] * share, axis=0)
        spot = (pl.ds(pl.multiple_of(lax.rem(t, groups) * 8, 8), 8), pl.ds(place(phase, t), width))
        out_ref[spot] = image
        for peer in tgt_peers:
            pltpu.make_async_remote_copy(
                src_ref=out_ref.at[spot],
                dst_ref=out_ref.at[spot],
                send_sem=osend.at[phase],
                recv_sem=orecv.at[phase],
                device_id={"tgt": peer},
                device_id_type=MESH,
            ).start()

    for iteration in range(ITERS):
        for c in range(CHUNKS):
            f_all(iteration, c).wait_send()
        for h in range(HALVES):
            g_all(iteration, h).wait_send()
    for phase in range(PHASES):
        all_pieces(phase, shares, lsend, lrecv).wait_send()
        all_pieces(phase, pieces, vsend, vrecv).wait_send()
        all_pieces(phase, pieces, osend, orecv).wait_recv()
        all_pieces(phase, pieces, osend, orecv).wait_send()


def store(f_in, g_in, out_in, f_out, g_out, out_out, sems):
    copies = [
        pltpu.make_async_copy(a, b, sems.at[k])
        for k, (a, b) in enumerate(((out_in, out_out), (f_in, f_out), (g_in, g_out)))
    ]
    for copy in copies:
        copy.start()
    for copy in copies:
        copy.wait()


def solution(mesh):
    n_src, n_tgt = mesh.shape["src"], mesh.shape["tgt"]

    def local(source_points, target_points, source_mass, target_mass, target_start):
        dim, rows = source_points.shape
        columns = target_points.shape[1]
        f32, bf16 = jnp.float32, jnp.bfloat16
        vmem = pl.BlockSpec(memory_space=pltpu.VMEM)
        hbm = pl.BlockSpec(memory_space=pltpu.HBM)
        dma = pltpu.SemaphoreType.DMA
        outs = (
            jax.ShapeDtypeStruct((1, rows), f32),
            jax.ShapeDtypeStruct((1, columns), f32),
            jax.ShapeDtypeStruct((dim, rows), f32),
        )
        chunk, span = rows // CHUNKS, columns // HALVES
        results = pl.pallas_call(
            functools.partial(
                kernel, n_src, n_tgt, math.log2(rows * n_src), math.log2(columns * n_tgt)
            ),
            out_shape=outs,
            in_specs=[hbm] * 5,
            out_specs=(vmem,) * 3,
            scratch_shapes=[
                pltpu.VMEM((dim, rows), bf16),
                pltpu.VMEM((dim, columns), bf16),
                pltpu.VMEM((1, rows), f32),
                pltpu.VMEM((1, columns), f32),
                pltpu.VMEM((1, columns), f32),
                pltpu.VMEM((DEPTH, rows), bf16),
                pltpu.VMEM((DEPTH, rows), bf16),
                pltpu.VMEM((DEPTH, columns), bf16),
                pltpu.VMEM((DEPTH, columns), bf16),
                pltpu.VMEM((1, rows), f32),
                pltpu.VMEM((1, columns), f32),
                pltpu.VMEM((8, rows), f32),
                pltpu.VMEM((8, rows), f32),
                pltpu.VMEM((8, columns), f32),
                pltpu.VMEM((8, columns), f32),
                pltpu.VMEM((ITERS, CHUNKS, n_tgt, 1, chunk), f32),
                pltpu.VMEM((ITERS, HALVES, n_src, 1, span), f32),
                pltpu.VMEM((dim // 8, 8, rows), f32),
                pltpu.VMEM((1, rows), f32),
                pltpu.VMEM((PHASES, n_tgt, 8, dim // 8 * rows // (PHASES * n_tgt)), f32),
                pltpu.VMEM((PHASES, n_tgt, 1, dim // 8 * rows // (PHASES * n_tgt)), f32),
                dma((5,)),
                dma((ITERS, CHUNKS)),
                dma((ITERS, CHUNKS)),
                dma((ITERS, HALVES)),
                dma((ITERS, HALVES)),
                dma((PHASES,)),
                dma((PHASES,)),
                dma((PHASES,)),
                dma((PHASES,)),
                dma((PHASES,)),
                dma((PHASES,)),
            ],
            compiler_params=pltpu.CompilerParams(
                collective_id=0, has_side_effects=True, vmem_limit_bytes=48 << 20
            ),
        )(
            *[pltpu.with_memory_space_constraint(v, pltpu.HBM) for v in (source_points, target_points, source_mass.reshape(1, rows), target_mass.reshape(1, columns), target_start.reshape(1, columns))]
        )
        f, g, mapped = pl.pallas_call(
            store,
            out_shape=outs,
            in_specs=[vmem] * 3,
            out_specs=(hbm,) * 3,
            scratch_shapes=[dma((3,))],
            compiler_params=pltpu.CompilerParams(vmem_limit_bytes=1 << 20),
        )(*results)
        return f.reshape(rows), g.reshape(columns), mapped

    placed = (P(None, "src"), P(None, "tgt"), P("src"), P("tgt"), P("tgt"))
    return jax.shard_map(
        local,
        mesh=mesh,
        in_specs=placed,
        out_specs=(P("src"), P("tgt"), P(None, "src")),
        check_vma=False,
    )
```

```python
import functools
import math

import jax
import jax.numpy as jnp
from jax import lax
from jax.experimental import pallas as pl
from jax.experimental.pallas import tpu as pltpu
from jax.sharding import PartitionSpec as P

ITERS = 2
MESH = pl.DeviceIdType.MESH
LOG2E = math.log2(math.e)
LN2 = math.log(2.0)
DEPTH = 128
CHUNKS = 2
HALVES = 1
PHASES = 2
MAPS = 4
TILE = 256


def far_first(n):
    return sorted(range(n), key=lambda d: -min(d, n - d))


def split3(value):
    high = value.astype(jnp.bfloat16).astype(jnp.float32)
    rest = value - high
    mid = rest.astype(jnp.bfloat16).astype(jnp.float32)
    return high, mid, rest - mid


def term_rows(value):
    n = value.shape[1]
    row = lax.broadcasted_iota(jnp.int32, (16, n), 0)
    high, mid, low = split3(value)
    block = jnp.where(row == 0, high, jnp.where(row == 1, mid, jnp.where(row == 2, low, 0.0)))
    return block.astype(jnp.bfloat16)


def one_rows(n):
    row = lax.broadcasted_iota(jnp.int32, (16, n), 0)
    return jnp.where(row < 3, 1.0, 0.0).astype(jnp.bfloat16)


def combine(values):
    top = jnp.max(values, axis=0)
    return top + jnp.log2(jnp.sum(jnp.exp2(values - top[None]), axis=0))


def scores(left, right):
    return lax.dot_general(
        left, right, (((0,), (0,)), ((), ())), preferred_element_type=jnp.float32
    )


def partial(block):
    n = block.shape[1]
    groups = block.reshape(block.shape[0] // 8, 8, n)
    top = jnp.max(groups, axis=0)
    return top, jnp.sum(jnp.exp2(groups - top[None]), axis=0)


def tiled(left, right, kept, reduced):
    tops, sums = [], []
    for a in range(kept.start, kept.stop, TILE):
        pair = None
        for b in range(reduced.start, reduced.stop, TILE):
            piece = partial(scores(left[:, b : b + TILE], right[:, a : a + TILE]))
            pair = piece if pair is None else merge(pair, piece)
        tops.append(pair[0])
        sums.append(pair[1])
    return jnp.concatenate(tops, axis=1), jnp.concatenate(sums, axis=1)


def merge(first, second):
    top = jnp.maximum(first[0], second[0])
    return top, first[1] * jnp.exp2(first[0] - top) + second[1] * jnp.exp2(second[0] - top)


def finish(pair):
    top = jnp.max(pair[0], axis=0, keepdims=True)
    return top + jnp.log2(jnp.sum(pair[1] * jnp.exp2(pair[0] - top), axis=0, keepdims=True))


def kernel(
    n_src, n_tgt, src_base, tgt_base,
    x_hbm, y_hbm, sm_hbm, tm_hbm, g0_hbm,
    f_ref, g_ref, out_ref,
    x_ref, y_ref, sm_ref, tm_ref, g0_ref,
    xr, xc, yr, yc, xsq, ysq, rtop, rsum, ctop, csum, fbuf, gbuf, vals, logs, pieces, shares,
    loads, fsend, frecv, gsend, grecv, vsend, vrecv, lsend, lrecv, osend, orecv,
):
    dim, rows = x_ref.shape
    columns = y_ref.shape[1]
    s = lax.axis_index("src")
    t = lax.axis_index("tgt")
    groups = dim // 8
    width = groups * rows // (PHASES * n_tgt)
    chunk = rows // CHUNKS
    span = columns // HALVES

    copies = [
        pltpu.make_async_copy(a, b, loads.at[k])
        for k, (a, b) in enumerate(
            (
                (x_hbm, x_ref),
                (y_hbm, y_ref),
                (sm_hbm, sm_ref),
                (tm_hbm, tm_ref),
                (g0_hbm, g0_ref),
            )
        )
    ]
    nx, ny, nz = 4, n_tgt // 4, n_src // 2
    xs = [lax.rem(t // ny + d, nx) * ny for d in far_first(nx)]
    ys = [lax.rem(lax.rem(t, ny) + d, ny) for d in far_first(ny)]
    zs = [lax.rem(s // 2 + d, nz) * 2 for d in far_first(nz)]
    cs = [1 - lax.rem(s, 2), lax.rem(s, 2)]
    tgt_peers = [b + a for a in ys for b in xs][:-1]
    src_peers = [b + a for b in zs for a in cs][:-1]

    barrier = pltpu.get_barrier_semaphore()
    for axis, peers in (("tgt", tgt_peers), ("src", src_peers)):
        for peer in peers:
            pl.semaphore_signal(barrier, inc=1, device_id={axis: peer}, device_id_type=MESH)
    for copy in copies:
        copy.start()
    for copy in copies:
        copy.wait()

    x = x_ref[...].astype(jnp.float32)
    y = y_ref[...].astype(jnp.float32)
    xsq[...] = jnp.sum(x * x, axis=0, keepdims=True)
    ysq[...] = jnp.sum(y * y, axis=0, keepdims=True)
    for k, part in enumerate(split3(x * (4.0 * LOG2E))):
        rounded = part.astype(jnp.bfloat16)
        at = slice(k * dim, (k + 1) * dim)
        xr[at, :] = rounded
        xc[at, :] = rounded
        yr[at, :] = y_ref[...]
        yc[at, :] = y_ref[...]
    used = 3 * dim
    extra = slice(used, used + 16)
    for ref in (xr, xc, yr, yc):
        ref[used:, :] = jnp.zeros((DEPTH - used, ref.shape[1]), jnp.bfloat16)
    xr[extra, :] = one_rows(rows)
    yc[extra, :] = one_rows(columns)

    def send_all(buf, me, axis, count, send, recv):
        for peer in tgt_peers if axis == "tgt" else src_peers:
            pltpu.make_async_remote_copy(
                src_ref=buf.at[me],
                dst_ref=buf.at[me],
                send_sem=send,
                recv_sem=recv,
                device_id={axis: peer},
                device_id_type=MESH,
            ).start()

    def whole(buf, count, axis, me, send, recv):
        part = buf.at[pl.ds(0, count - 1)]
        return pltpu.make_async_remote_copy(
            src_ref=part,
            dst_ref=part,
            send_sem=send,
            recv_sem=recv,
            device_id={axis: lax.rem(me + 1, count)},
            device_id_type=MESH,
        )

    def f_all(i, c):
        return whole(fbuf.at[i, c], n_tgt, "tgt", t, fsend.at[i, c], frecv.at[i, c])

    def g_all(i, h):
        return whole(gbuf.at[i, h], n_src, "src", s, gsend.at[i, h], grecv.at[i, h])

    for iteration in range(ITERS):
        for h in range(HALVES):
            cols = slice(h * span, (h + 1) * span)
            if iteration == 0:
                terms = (
                    LOG2E * (2.0 * g0_ref[:, cols] + tm_ref[:, cols] - 2.0 * ysq[:, cols])
                    - tgt_base
                )
            else:
                g_all(iteration - 1, h).wait_recv()
                terms = LOG2E * tm_ref[:, cols] - tgt_base - combine(gbuf[iteration - 1, h])
            yr[extra, cols] = term_rows(terms)
            for c in range(CHUNKS):
                at = slice(c * chunk, (c + 1) * chunk)
                pair = tiled(yr, xr, at, cols)
                if h > 0:
                    pair = merge((rtop[:, at], rsum[:, at]), pair)
                if h < HALVES - 1:
                    rtop[:, at], rsum[:, at] = pair
                else:
                    fbuf[iteration, c, t] = finish(pair)
                    if iteration > 0:
                        send_all(
                            fbuf.at[iteration, c], t, "tgt", n_tgt,
                            fsend.at[iteration, c], frecv.at[iteration, c],
                        )
        if iteration == 0:
            pl.semaphore_wait(barrier, n_src + n_tgt - 2)
            for peer in tgt_peers:
                for c in range(CHUNKS):
                    pltpu.make_async_remote_copy(
                        src_ref=fbuf.at[iteration, c, t],
                        dst_ref=fbuf.at[iteration, c, t],
                        send_sem=fsend.at[iteration, c],
                        recv_sem=frecv.at[iteration, c],
                        device_id={"tgt": peer},
                        device_id_type=MESH,
                    ).start()
        for c in range(CHUNKS):
            at = slice(c * chunk, (c + 1) * chunk)
            f_all(iteration, c).wait_recv()
            row_lse = combine(fbuf[iteration, c])
            if iteration == ITERS - 1:
                f_ref[:, at] = xsq[:, at] - (0.5 * LN2) * row_lse
            xc[extra, at] = term_rows(LOG2E * sm_ref[:, at] - src_base - row_lse)
            for h in range(HALVES):
                cols = slice(h * span, (h + 1) * span)
                pair = tiled(xc, yc, cols, at)
                if c > 0:
                    pair = merge((ctop[:, cols], csum[:, cols]), pair)
                if c < CHUNKS - 1:
                    ctop[:, cols], csum[:, cols] = pair
                else:
                    gbuf[iteration, h, s] = finish(pair)
                    send_all(
                        gbuf.at[iteration, h], s, "src", n_src,
                        gsend.at[iteration, h], grecv.at[iteration, h],
                    )

    for h in range(HALVES):
        cols = slice(h * span, (h + 1) * span)
        g_all(ITERS - 1, h).wait_recv()
        column_lse = combine(gbuf[ITERS - 1, h])
        g_ref[:, cols] = ysq[:, cols] - (0.5 * LN2) * column_lse
        yr[extra, cols] = term_rows(LOG2E * tm_ref[:, cols] - tgt_base - column_lse)

    def place(phase, p):
        return pl.multiple_of(phase * (rows // PHASES) + p // groups * width, width)

    piece = rows // MAPS
    for phase in range(PHASES):
        for turn in range(2):
            k = lax.rem(t // (n_tgt // 2) + 1 + turn, 2)
            at = pl.ds(pl.multiple_of((2 * phase + k) * piece, piece), piece)
            block = scores(yr[...], xr[:, at])
            top = jnp.max(block, axis=0, keepdims=True)
            weights = jnp.exp2(block - top)
            total = jnp.sum(weights, axis=0, keepdims=True)
            summed = lax.dot_general(
                y_ref[...],
                weights.astype(jnp.bfloat16),
                (((1,), (0,)), ((), ())),
                preferred_element_type=jnp.float32,
            )
            mean = summed / total
            for q in range(groups):
                vals[q, :, at] = mean[q * 8 : (q + 1) * 8]
            logs[:, at] = top + jnp.log2(total)
            near = [2 * ny * k + ny * r for r in (1 - lax.rem(t // ny, 2), lax.rem(t // ny, 2))]
            owners = [b + a for a in ys for b in near]
            for p in owners[:-1] if turn == 1 else owners:
                lanes = pl.ds(place(phase, p), width)
                for source, target, send, recv in (
                    (vals.at[lax.rem(p, groups), :, lanes], pieces, vsend, vrecv),
                    (logs.at[:, lanes], shares, lsend, lrecv),
                ):
                    pltpu.make_async_remote_copy(
                        src_ref=source,
                        dst_ref=target.at[phase, t],
                        send_sem=send.at[phase],
                        recv_sem=recv.at[phase],
                        device_id={"tgt": p},
                        device_id_type=MESH,
                    ).start()

    def all_pieces(phase, ref, send, recv):
        part = ref.at[phase, pl.ds(0, n_tgt - 1)]
        return pltpu.make_async_remote_copy(
            src_ref=part,
            dst_ref=part,
            send_sem=send.at[phase],
            recv_sem=recv.at[phase],
            device_id={"tgt": tgt_peers[0]},
            device_id_type=MESH,
        )

    for phase in range(PHASES):
        pieces[phase, t] = vals[lax.rem(t, groups), :, pl.ds(place(phase, t), width)]
        shares[phase, t] = logs[:, pl.ds(place(phase, t), width)]
        all_pieces(phase, shares, lsend, lrecv).wait_recv()
        lse = shares[phase]
        top = jnp.max(lse, axis=0, keepdims=True)
        share = jnp.exp2(lse - top)
        share = share / jnp.sum(share, axis=0, keepdims=True)
        all_pieces(phase, pieces, vsend, vrecv).wait_recv()
        image = jnp.sum(pieces[phase] * share, axis=0)
        spot = (pl.ds(pl.multiple_of(lax.rem(t, groups) * 8, 8), 8), pl.ds(place(phase, t), width))
        out_ref[spot] = image
        for peer in tgt_peers:
            pltpu.make_async_remote_copy(
                src_ref=out_ref.at[spot],
                dst_ref=out_ref.at[spot],
                send_sem=osend.at[phase],
                recv_sem=orecv.at[phase],
                device_id={"tgt": peer},
                device_id_type=MESH,
            ).start()

    for iteration in range(ITERS):
        for c in range(CHUNKS):
            f_all(iteration, c).wait_send()
        for h in range(HALVES):
            g_all(iteration, h).wait_send()
    for phase in range(PHASES):
        all_pieces(phase, shares, lsend, lrecv).wait_send()
        all_pieces(phase, pieces, vsend, vrecv).wait_send()
        all_pieces(phase, pieces, osend, orecv).wait_recv()
        all_pieces(phase, pieces, osend, orecv).wait_send()


def store(f_in, g_in, out_in, f_out, g_out, out_out, sems):
    copies = [
        pltpu.make_async_copy(a, b, sems.at[k])
        for k, (a, b) in enumerate(((out_in, out_out), (f_in, f_out), (g_in, g_out)))
    ]
    for copy in copies:
        copy.start()
    for copy in copies:
        copy.wait()


def solution(mesh):
    n_src, n_tgt = mesh.shape["src"], mesh.shape["tgt"]

    def local(source_points, target_points, source_mass, target_mass, target_start):
        dim, rows = source_points.shape
        columns = target_points.shape[1]
        f32, bf16 = jnp.float32, jnp.bfloat16
        vmem = pl.BlockSpec(memory_space=pltpu.VMEM)
        hbm = pl.BlockSpec(memory_space=pltpu.HBM)
        dma = pltpu.SemaphoreType.DMA
        outs = (
            jax.ShapeDtypeStruct((1, rows), f32),
            jax.ShapeDtypeStruct((1, columns), f32),
            jax.ShapeDtypeStruct((dim, rows), f32),
        )
        chunk, span = rows // CHUNKS, columns // HALVES
        results = pl.pallas_call(
            functools.partial(
                kernel, n_src, n_tgt, math.log2(rows * n_src), math.log2(columns * n_tgt)
            ),
            out_shape=outs,
            in_specs=[hbm] * 5,
            out_specs=(vmem,) * 3,
            scratch_shapes=[
                pltpu.VMEM((dim, rows), bf16),
                pltpu.VMEM((dim, columns), bf16),
                pltpu.VMEM((1, rows), f32),
                pltpu.VMEM((1, columns), f32),
                pltpu.VMEM((1, columns), f32),
                pltpu.VMEM((DEPTH, rows), bf16),
                pltpu.VMEM((DEPTH, rows), bf16),
                pltpu.VMEM((DEPTH, columns), bf16),
                pltpu.VMEM((DEPTH, columns), bf16),
                pltpu.VMEM((1, rows), f32),
                pltpu.VMEM((1, columns), f32),
                pltpu.VMEM((8, rows), f32),
                pltpu.VMEM((8, rows), f32),
                pltpu.VMEM((8, columns), f32),
                pltpu.VMEM((8, columns), f32),
                pltpu.VMEM((ITERS, CHUNKS, n_tgt, 1, chunk), f32),
                pltpu.VMEM((ITERS, HALVES, n_src, 1, span), f32),
                pltpu.VMEM((dim // 8, 8, rows), f32),
                pltpu.VMEM((1, rows), f32),
                pltpu.VMEM((PHASES, n_tgt, 8, dim // 8 * rows // (PHASES * n_tgt)), f32),
                pltpu.VMEM((PHASES, n_tgt, 1, dim // 8 * rows // (PHASES * n_tgt)), f32),
                dma((5,)),
                dma((ITERS, CHUNKS)),
                dma((ITERS, CHUNKS)),
                dma((ITERS, HALVES)),
                dma((ITERS, HALVES)),
                dma((PHASES,)),
                dma((PHASES,)),
                dma((PHASES,)),
                dma((PHASES,)),
                dma((PHASES,)),
                dma((PHASES,)),
            ],
            compiler_params=pltpu.CompilerParams(
                collective_id=0, has_side_effects=True, vmem_limit_bytes=48 << 20
            ),
        )(
            *[pltpu.with_memory_space_constraint(v, pltpu.HBM) for v in (source_points, target_points, source_mass.reshape(1, rows), target_mass.reshape(1, columns), target_start.reshape(1, columns))]
        )
        f, g, mapped = pl.pallas_call(
            store,
            out_shape=outs,
            in_specs=[vmem] * 3,
            out_specs=(hbm,) * 3,
            scratch_shapes=[dma((3,))],
            compiler_params=pltpu.CompilerParams(vmem_limit_bytes=1 << 20),
        )(*results)
        return f.reshape(rows), g.reshape(columns), mapped

    placed = (P(None, "src"), P(None, "tgt"), P("src"), P("tgt"), P("tgt"))
    return jax.shard_map(
        local,
        mesh=mesh,
        in_specs=placed,
        out_specs=(P("src"), P("tgt"), P(None, "src")),
        check_vma=False,
    )
```
